32 devices in a mesh: bands: 2 (over core), gy: 4 (over y, x), gz: 4 (over z).
Axes of the slice: x: 2, y: 2, z: 4, core: 2. Of those that a mesh axis runs over, the one named last changes fastest.
Arguments:
- orbitals: float32 [4, 64, 64, 128], P('bands', 'gy', 'gz'), may hold values from -6 to 6
- orbital_shift: float32 [4], P('bands'), may hold values from 0.1 to 1
- occupation: float32 [4], P('bands'), may hold values from 0.125 to 0.5
- potential: float32 [64, 64, 128], P('gy', 'gz'), may hold values from 0.1 to 2
- perturbation: float32 [64, 64, 128], P('gy', 'gz'), may hold values from -6 to 6
- kernel: float32 [64, 64, 128], P('gy', 'gz'), may hold values from 0.2 to 1
Outputs:
- response: float32 [4, 64, 64, 128], P('bands', 'gy', 'gz')
- density: float32 [64, 64, 128], P('gy', 'gz', 'bands')
The draws below stay inside these ranges and needn't reach their ends.
All inputs are finite; a program needn't handle non-finite values.
Results may differ from the reference program's by a relative error of at most 0.00002.
Values sent between devices are 32-bit elements; how exact they have to be, the bound alone decides.
A program may use at most 64 MiB of HBM per device.

```python
import math
import jax
import jax.numpy as jnp
from jax import lax

NX = 128
SWEEPS = 4
OUTER = 2
ORBS = 4
NY = 64
NZ = 64


def block_scale(key, dims, cuts, low, high):
    level, own = 1.0, jax.random.fold_in(key, 6)
    for axis_at, shards_of in cuts:
        heights = jnp.exp(jax.random.uniform(jax.random.fold_in(own, axis_at), (shards_of,), jnp.float32, low / len(cuts), high / len(cuts)))
        level = level * jnp.repeat(heights, dims[axis_at] // shards_of).reshape([-1 if axis == axis_at else 1 for axis in range(len(dims))])
    return level


def centred(stream_key, extent, scale, limit, shards=(), held_as=jnp.bfloat16):
    gain = block_scale(stream_key, extent, shards, -0.22, 0.18) if shards else 1.0
    array = jax.random.normal(stream_key, extent, jnp.float32) * scale * gain
    return jnp.minimum(jnp.maximum(array, -limit), limit).astype(held_as)


def setup_inputs(seed: int = 0) -> dict:
    splits = jax.random.split(jax.random.key(seed), 7)
    orbitals = centred(splits[0], (ORBS, NY, NZ, NX), 1.0, 6.0, ((0, 2), (1, 4), (2, 4)), jnp.float32)
    orbital_shift = jnp.clip(jnp.exp(math.log(1.0) - 2.3025851 * jax.random.uniform(splits[1], (ORBS,), jnp.float32) ** block_scale(splits[1], (ORBS,), ((0, 2),), -0.2, 0.2)), 0.1, 1.0)
    occupation = jnp.clip(0.125 + 0.375 * jax.random.uniform(splits[2], (ORBS,), jnp.float32) ** block_scale(splits[2], (ORBS,), ((0, 2),), -0.2, 0.2), 0.125, 0.5)
    potential = jnp.clip(jnp.exp(math.log(2.0) - 2.9957323 * jax.random.uniform(splits[3], (NY, NZ, NX), jnp.float32) ** block_scale(splits[3], (NY, NZ, NX), ((0, 4), (1, 4)), -0.2, 0.2)), 0.1, 2.0)
    perturbation = centred(splits[4], (NY, NZ, NX), 1.0, 6.0, ((0, 4), (1, 4)), jnp.float32)
    kernel = jnp.clip(0.2 + 0.8 * jax.random.uniform(splits[5], (NY, NZ, NX), jnp.float32) ** block_scale(splits[5], (NY, NZ, NX), ((0, 4), (1, 4)), -0.2, 0.2), 0.2, 1.0)
    return dict(orbitals=orbitals, orbital_shift=orbital_shift, occupation=occupation, potential=potential, perturbation=perturbation, kernel=kernel)


relax_factor = 0.8


def roll_sum(field):
    return jnp.roll(field, 1, -1) + jnp.roll(field, -1, -1)


def laplace_parts(padded):
    centre = padded[..., 1:-1, 1:-1, :]
    along_y = padded[..., 2:, 1:-1, :] + padded[..., :-2, 1:-1, :]
    along_z = padded[..., 1:-1, 2:, :] + padded[..., 1:-1, :-2, :]
    plane_corners = padded[..., 2:, 2:, :] + padded[..., 2:, :-2, :] + padded[..., :-2, 2:, :] + padded[..., :-2, :-2, :]
    face_sum = roll_sum(centre) + along_y + along_z
    edge_sum = roll_sum(along_y) + roll_sum(along_z) + plane_corners
    corner_sum = roll_sum(plane_corners)
    laplacian = (-128.0 * centre + 14.0 * face_sum + 3.0 * edge_sum + corner_sum) / 30.0
    return centre, laplacian


def mehrstellen(padded):
    centre = padded[..., 1:-1, 1:-1, :]
    along_y = padded[..., 2:, 1:-1, :] + padded[..., :-2, 1:-1, :]
    along_z = padded[..., 1:-1, 2:, :] + padded[..., 1:-1, :-2, :]
    return 0.5 * centre + (roll_sum(centre) + along_y + along_z) / 12.0


def relax(padded, weight, source):
    centre, laplacian = laplace_parts(padded)
    diagonal = 32.0 / 15.0 + weight
    applied = -0.5 * laplacian + weight * centre
    return centre + relax_factor * (source - applied) / diagonal


def wrapped(field):
    return jnp.pad(field, ((1, 1), (1, 1), (0, 0)), mode="wrap")


def reference(orbitals, orbital_shift, occupation, potential, perturbation, kernel):
    change = perturbation
    response = jnp.zeros_like(orbitals)
    density = jnp.zeros_like(potential)
    for update in range(OUTER):
        def relax_orbital(accumulated, element):
            orbital, shift_value, weight_value, field = element
            weight = potential + shift_value
            source = -mehrstellen(wrapped(change * orbital))
            for sweep_index in range(SWEEPS):
                field = relax(wrapped(field), weight, source)
            return accumulated + weight_value * orbital * field, field

        density, response = lax.scan(relax_orbital, jnp.zeros_like(potential), (orbitals, orbital_shift, occupation, response))
        if update + 1 < OUTER:
            change = perturbation + kernel * density
    return response, density
```

```python
import functools

import jax
import jax.numpy as jnp
from jax import lax
from jax.experimental import pallas as pl
from jax.experimental.pallas import tpu as pltpu
from jax.sharding import PartitionSpec as P

SWEEPS = 4
OUTER = 2
RELAX = 0.8
MESH = pl.DeviceIdType.MESH
CHUNK = 32
GRANT = 24 * 1024 * 1024


def chunks(start, stop, size):
    row = start
    while row < stop:
        step = min(size, stop - row)
        yield row, step
        row += step


def kernel(counts, shift_hbm, occ_hbm, orb_hbm, pot_hbm, pert_hbm, kern_hbm,
           respv, dens_ref,
           shift_ref, occ_ref, orb_ref, pp_ref, kern_ref,
           zs1, yr1, zr1, zsu, yr2, zr2, resp0, part, partr, part2, partr2, hp, hpr,
           obuf, fbuf, rbuf, sbuf, ua, ub, pbuf,
           send1, recv1, send2, recv2, sendb, recvb, local_sem):
    nb, gy, gz = counts
    w = SWEEPS
    orbs, ny, nz, nx = orb_ref.shape
    zp = nz + 2 * w
    yp_count = ny + 2 * w
    base = zp + 8
    b = lax.axis_index("bands")
    y = lax.axis_index("gy")
    z = lax.axis_index("gz")
    parity = lax.rem(b, 2)
    ysides = {1: lax.rem(y + 1, gy), -1: lax.rem(y + gy - 1, gy), 0: y}
    zsides = {1: lax.rem(z + 1, gz), -1: lax.rem(z + gz - 1, gz), 0: z}

    def device(dy, dz):
        return {"bands": b, "gy": ysides[dy], "gz": zsides[dz]}

    faces = ((0, 1), (0, -1), (1, 0), (-1, 0))
    corners = ((1, 1), (1, -1), (-1, 1), (-1, -1))
    barrier = pltpu.get_barrier_semaphore()
    for dy, dz in corners + faces:
        pl.semaphore_signal(barrier, inc=1, device_id=device(dy, dz), device_id_type=MESH)
    for d in range(1, nb):
        pl.semaphore_signal(barrier, inc=1, device_id={"bands": lax.rem(b + d, nb), "gy": y, "gz": z},
                            device_id_type=MESH)
    loads = [pltpu.make_async_copy(src, dst, local_sem.at[i]) for i, (src, dst) in enumerate((
        (pert_hbm, pp_ref.at[0]), (pot_hbm, pp_ref.at[1]), (orb_hbm, orb_ref), (kern_hbm, kern_ref),
        (shift_hbm, shift_ref), (occ_hbm, occ_ref)))]
    for copy in loads:
        copy.start()

    def pack(dst, slot, value_of):
        for row in range(ny):
            dst[0, slot, row * w:(row + 1) * w, :] = value_of(row, 0)
            dst[1, slot, row * w:(row + 1) * w, :] = value_of(row, nz - w)

    def border(packed, slots, own, yr, zr, send, recv, at):
        made = {}
        for dy, dz in faces + corners:
            n = at + len(made)
            if dz:
                side, into = (1, 0) if dz == 1 else (0, 1)
                if dy == 1:
                    src, dst, size = (ny - w) * w, 8, w * w
                elif dy == -1:
                    src, dst, size = 0, 8 + (w + ny) * w, w * w
                else:
                    src, dst, size = 0, 8 + w * w, ny * w
                source = packed.at[side, slots, pl.ds(src, size)]
                target = zr.at[into, slots, pl.ds(dst, size)]
            else:
                into, start = (0, ny - w) if dy == 1 else (1, 0)
                source = own(start)
                target = yr.at[into, slots]
            made[dy, dz] = pltpu.make_async_remote_copy(
                src_ref=source, dst_ref=target, send_sem=send.at[n], recv_sem=recv.at[n],
                device_id=device(dy, dz), device_id_type=MESH)
        return made

    pslot, vslot, kslot = orbs, orbs + 1, orbs + 2
    mine = orbs + parity
    loads[0].wait()
    pack(zs1, pslot, lambda row, at: pp_ref[0, row, at:at + w, :])
    loads[1].wait()
    pack(zs1, vslot, lambda row, at: pp_ref[1, row, at:at + w, :])
    loads[2].wait()
    for o in range(orbs):
        pack(zs1, o, lambda row, at, o=o: orb_ref[o, row, at:at + w, :])
    loads[3].wait()
    pack(zs1, kslot, lambda row, at: kern_ref[row, at:at + w, :])
    loads[4].wait()
    loads[5].wait()
    pl.semaphore_wait(barrier, len(faces + corners) + nb - 1)

    own_mine = border(zs1, mine, lambda start: pp_ref.at[parity, pl.ds(start, w)], yr1, zr1, send1, recv1, 0)
    own_orbs = border(zs1, pl.ds(0, orbs), lambda start: orb_ref.at[:, pl.ds(start, w)], yr1, zr1, send1, recv1, 8)
    for key in corners:
        own_orbs[key].start()
    for key in corners + faces:
        own_mine[key].start()
    for key in faces:
        own_orbs[key].start()

    sign = 1 - 2 * parity
    partner = {"bands": b + sign, "gy": y, "gz": z}
    ysend = lax.rem(y + gy + sign, gy)
    zsend = lax.rem(z + gz + sign, gz)
    source_row = pl.multiple_of((1 - parity) * ((ny - w) * w), 8)
    target_row = pl.multiple_of(8 + parity * ((w + ny) * w), 8)
    moves = (
        (zs1.at[1, kslot, pl.ds(source_row, w * w)], zr1.at[0, kslot, pl.ds(target_row, w * w)], ysend, zsides[1]),
        (zs1.at[0, kslot, pl.ds(source_row, w * w)], zr1.at[1, kslot, pl.ds(target_row, w * w)], ysend, zsides[-1]),
        (zs1.at[1 - parity, kslot], zr1.at[parity, kslot, pl.ds(8 + w * w, ny * w)], y, zsend),
        (kern_ref.at[pl.ds((1 - parity) * (ny - w), w)], yr1.at[parity, kslot], ysend, z),
    )
    kern_copies = [pltpu.make_async_remote_copy(
        src_ref=src, dst_ref=dst, send_sem=send1.at[16 + i], recv_sem=recv1.at[16 + i],
        device_id={"bands": b, "gy": ty, "gz": tz}, device_id_type=MESH)
        for i, (src, dst, ty, tz) in enumerate(moves)]
    kern_relays = [pltpu.make_async_remote_copy(
        src_ref=dst, dst_ref=dst, send_sem=send1.at[20 + i], recv_sem=recv1.at[20 + i],
        device_id=partner, device_id_type=MESH) for i, (_, dst, _, _) in enumerate(moves)]
    for copy in kern_copies:
        copy.start()
    for key in faces + corners:
        own_mine[key].wait_recv()
    relays = [pltpu.make_async_remote_copy(
        src_ref=ref.at[:, mine], dst_ref=ref.at[:, mine], send_sem=send1.at[24 + i], recv_sem=recv1.at[24 + i],
        device_id=partner, device_id_type=MESH) for i, ref in enumerate((yr1, zr1))]
    for copy in relays:
        copy.start()
    for copy in relays:
        copy.wait_recv()
    for key in faces + corners:
        own_orbs[key].wait_recv()

    low = lax.broadcasted_iota(jnp.int32, (8, nx), 0) < w

    def tiles():
        for yp in range(-1, yp_count):
            if yp >= 0:
                yield yp, 0, base + zp * yp, nz
            yield yp, 1, base + zp * yp + nz, 2 * w

    def padded(own, yr, zr, slot, yp, third):
        if third:
            row = 8 + w * yp
            return jnp.where(low, zr[1, slot, row:row + 2 * w, :], zr[0, slot, row:row + 2 * w, :])
        if yp < w:
            return yr[0, slot, yp]
        if yp >= w + ny:
            return yr[1, slot, yp - w - ny]
        return own(yp - w)

    for yp, third, row, size in tiles():
        pv = padded(lambda r: pp_ref[0, r], yr1, zr1, pslot, yp, third)
        vv = padded(lambda r: pp_ref[1, r], yr1, zr1, vslot, yp, third)
        pbuf[row:row + size, :] = pv
        for o in range(orbs):
            ov = padded(lambda r: orb_ref[o, r], yr1, zr1, o, yp, third)
            obuf[o, row:row + size, :] = ov
            fbuf[o, row:row + size, :] = ov * pv
            rbuf[o, row:row + size, :] = (RELAX / 60.0) / (32.0 / 15.0 + (vv + shift_ref[o]))

    def span(k):
        return base + zp * (k - 1) + nz, base + zp * (yp_count - k)

    def lane_sum(v):
        return pltpu.roll(v, 1, 1) + pltpu.roll(v, nx - 1, 1)

    def source60(o, row, size):
        def at(shift):
            return fbuf[o, row + shift:row + shift + size, :]
        f = at(0)
        return -30.0 * f - 5.0 * (lane_sum(f) + (at(zp) + at(-zp)) + (at(1) + at(-1)))

    def relaxed(u, o, row, size, source):
        def at(shift):
            return u[o, row + shift:row + shift + size, :]
        c = at(0)
        faces = (at(zp) + at(-zp)) + (at(1) + at(-1))
        corners = (at(zp + 1) + at(zp - 1)) + (at(1 - zp) + at(-1 - zp))
        off = 14.0 * faces + 3.0 * corners + lane_sum(14.0 * c + 3.0 * faces + corners)
        return 0.2 * c + rbuf[o, row:row + size, :] * (source + off)

    def sweep(src, dst, k):
        for o in range(orbs):
            for row, size in chunks(*span(k), CHUNK):
                dst[o, row:row + size, :] = relaxed(src, o, row, size, sbuf[o, row:row + size, :])

    def last(src, dst, part_ref):
        for o in range(orbs):
            for r in range(ny):
                row = base + zp * (r + w)
                value = relaxed(src, o, row, nz, sbuf[o, row:row + nz, :])
                dst[o, r] = value
                term = occ_ref[o] * obuf[o, row:row + nz, :] * value
                part_ref[r] = term if o == 0 else part_ref[r] + term

    def band_copies(src, dst, at):
        return [pltpu.make_async_remote_copy(
            src_ref=src, dst_ref=dst.at[d - 1], send_sem=sendb.at[at + d - 1], recv_sem=recvb.at[at + d - 1],
            device_id={"bands": lax.rem(b + d, nb), "gy": y, "gz": z}, device_id_type=MESH)
            for d in range(1, nb)]

    for o in range(orbs):
        for row, size in chunks(*span(1), CHUNK):
            s = source60(o, row, size)
            sbuf[o, row:row + size, :] = s
            ua[o, row:row + size, :] = rbuf[o, row:row + size, :] * s
    sweep(ua, ub, 2)
    sweep(ub, ua, 3)
    last(ua, resp0, part)

    bands = band_copies(part, partr, 0)
    for copy in bands:
        copy.start()
    for o in range(orbs):
        pack(zsu, o, lambda row, at, o=o: resp0[o, row, at:at + w, :])
    second = border(zsu, pl.ds(0, orbs), lambda start: resp0.at[:, pl.ds(start, w)], yr2, zr2, send2, recv2, 0)
    for key in corners + faces:
        second[key].start()
    for copy in bands:
        copy.wait_recv()
    for copy in kern_copies:
        copy.wait_recv()
    for copy in kern_relays:
        copy.start()
    for r in range(ny):
        total = part[r]
        for d in range(nb - 1):
            total = total + partr[d, r]
        row = base + zp * (r + w)
        cv = pbuf[row:row + nz, :] + kern_ref[r] * total
        for o in range(orbs):
            fbuf[o, row:row + nz, :] = obuf[o, row:row + nz, :] * cv
            ua[o, row:row + nz, :] = resp0[o, r]
    for copy in kern_relays:
        copy.wait_recv()
    for key in faces + corners:
        second[key].wait_recv()

    rim, at = [], 0
    for yp, third, row, size in tiles():
        if third or yp < w or yp >= w + ny:
            rim.append((yp, third, row, size, at))
            at += size
    for yp, third, row, size, at in rim:
        term = None
        for o in range(orbs):
            value = padded(None, yr2, zr2, o, yp, third)
            ua[o, row:row + size, :] = value
            more = occ_ref[o] * obuf[o, row:row + size, :] * value
            term = more if term is None else term + more
        hp[at:at + size, :] = term
    rims = band_copies(hp, hpr, 2 * (nb - 1))
    for copy in rims:
        copy.start()
    for copy in rims:
        copy.wait_recv()
    for yp, third, row, size, at in rim:
        total = hp[at:at + size, :]
        for d in range(nb - 1):
            total = total + hpr[d, at:at + size, :]
        cv = pbuf[row:row + size, :] + padded(None, yr1, zr1, kslot, yp, third) * total
        for o in range(orbs):
            fbuf[o, row:row + size, :] = obuf[o, row:row + size, :] * cv
    for o in range(orbs):
        for row, size in chunks(*span(1), CHUNK):
            s = source60(o, row, size)
            sbuf[o, row:row + size, :] = s
            ub[o, row:row + size, :] = relaxed(ua, o, row, size, s)
    sweep(ub, ua, 2)
    sweep(ua, ub, 3)
    last(ub, respv, part2)
    bands2 = band_copies(part2, partr2, nb - 1)
    for copy in bands2:
        copy.start()
    for copy in bands2:
        copy.wait_recv()
    width = nx // nb
    for r in range(ny):
        total = part2[r]
        for d in range(nb - 1):
            total = total + partr2[d, r]
        dens_ref[r] = pltpu.roll(total, lax.rem(nx - b * width, nx), 1)[:, :width]
    for group in (own_mine, own_orbs, second):
        for key in faces + corners:
            group[key].wait_send()
    for copy in relays + kern_copies + kern_relays + bands + rims + bands2:
        copy.wait_send()


def store(resp_ref, dens_ref, resp_hbm, dens_hbm, sem):
    copies = [pltpu.make_async_copy(src, dst, sem.at[i])
              for i, (src, dst) in enumerate(((resp_ref, resp_hbm), (dens_ref, dens_hbm)))]
    for copy in copies:
        copy.start()
    for copy in copies:
        copy.wait()


def on_device(counts, orbitals, orbital_shift, occupation, potential, perturbation, kernel_field):
    nb = counts[0]
    orbs, ny, nz, nx = orbitals.shape
    w = SWEEPS
    zp, yp_count = nz + 2 * w, ny + 2 * w
    rows = (nz + 2 * w) * (ny + 2 * w + 1) + 8 + 16
    rows = (rows + 7) // 8 * 8
    zrows = 8 + w * (ny + 2 * w) + 8
    f32 = jnp.float32
    vmem = lambda *shape: pltpu.VMEM(shape, f32)
    wide = vmem(orbs, rows, nx)
    tile = vmem(ny, nz, nx)
    dma = lambda n: pltpu.SemaphoreType.DMA((n,))
    rim_rows = (zp * yp_count - ny * nz) + 8
    scratch = [
        pltpu.SMEM((orbs,), f32), pltpu.SMEM((orbs,), f32),
        vmem(orbs, ny, nz, nx), vmem(2, ny, nz, nx), tile,
        vmem(2, orbs + 3, ny * w, nx), vmem(2, orbs + 3, w, nz, nx), vmem(2, orbs + 3, zrows, nx),
        vmem(2, orbs, ny * w, nx), vmem(2, orbs, w, nz, nx), vmem(2, orbs, zrows, nx),
        vmem(orbs, ny, nz, nx), tile, vmem(nb - 1, ny, nz, nx), tile, vmem(nb - 1, ny, nz, nx),
        vmem(rim_rows, nx), vmem(nb - 1, rim_rows, nx),
        wide, wide, wide, wide, wide, wide, vmem(rows, nx),
        dma(26), dma(26), dma(8), dma(8), dma(3 * (nb - 1)), dma(3 * (nb - 1)), dma(6),
    ]
    spec = pl.BlockSpec(memory_space=pltpu.VMEM)
    hbm = pl.BlockSpec(memory_space=pltpu.HBM)
    response, density = pl.pallas_call(
        functools.partial(kernel, counts),
        out_shape=(pltpu.VMEM(orbitals.shape, f32), pltpu.VMEM((ny, nz, nx // nb), f32)),
        in_specs=[hbm] * 6,
        out_specs=(spec, spec),
        scratch_shapes=scratch,
        compiler_params=pltpu.CompilerParams(
            collective_id=0, has_side_effects=True, vmem_limit_bytes=GRANT),
    )(*(pltpu.with_memory_space_constraint(array, pltpu.HBM) for array in (
        orbital_shift, occupation, orbitals, potential, perturbation, kernel_field)))
    return pl.pallas_call(
        store,
        out_shape=(jax.ShapeDtypeStruct(response.shape, f32), jax.ShapeDtypeStruct(density.shape, f32)),
        in_specs=[spec, spec],
        out_specs=(hbm, hbm),
        scratch_shapes=[dma(2)],
        compiler_params=pltpu.CompilerParams(vmem_limit_bytes=GRANT),
    )(response, density)


def solution(mesh):
    counts = (mesh.shape["bands"], mesh.shape["gy"], mesh.shape["gz"])
    placed = (
        P("bands", "gy", "gz", None),
        P("bands"),
        P("bands"),
        P("gy", "gz", None),
        P("gy", "gz", None),
        P("gy", "gz", None),
    )
    return jax.shard_map(
        functools.partial(on_device, counts),
        mesh=mesh,
        in_specs=placed,
        out_specs=(P("bands", "gy", "gz", None), P("gy", "gz", "bands")),
        check_vma=False,
    )
```

```python
import functools

import jax
import jax.numpy as jnp
from jax import lax
from jax.experimental import pallas as pl
from jax.experimental.pallas import tpu as pltpu
from jax.sharding import PartitionSpec as P

SWEEPS = 4
OUTER = 2
RELAX = 0.8
MESH = pl.DeviceIdType.MESH
CHUNK = 32
GRANT = 24 * 1024 * 1024


def chunks(start, stop, size):
    row = start
    while row < stop:
        step = min(size, stop - row)
        yield row, step
        row += step


def kernel(counts, shift_hbm, occ_hbm, orb_hbm, pot_hbm, pert_hbm, kern_hbm,
           respv, dens_ref,
           shift_ref, occ_ref, orb_ref, pp_ref, kern_ref,
           zs1, yr1, zr1, cs1, zsu, yr2, zr2, resp0, part, partr, part2, partr2, hp, hpr,
           obuf, fbuf, rbuf, sbuf, ua, ub, pbuf,
           send, recv, sendb, recvb, local_sem):
    nb, gy, gz = counts
    w = SWEEPS
    orbs, ny, nz, nx = orb_ref.shape
    zp = nz + 2 * w
    yp_count = ny + 2 * w
    base = zp + 8
    block = w * w
    first, top, bottom = 8 + block, 8, 8 + (w + ny) * w
    b = lax.axis_index("bands")
    y = lax.axis_index("gy")
    z = lax.axis_index("gz")
    parity = lax.rem(b, 2)
    ysides = {1: lax.rem(y + 1, gy), -1: lax.rem(y + gy - 1, gy), 0: y}
    zsides = {1: lax.rem(z + 1, gz), -1: lax.rem(z + gz - 1, gz), 0: z}

    def device(dy, dz):
        return {"bands": b, "gy": ysides[dy], "gz": zsides[dz]}

    faces = ((0, 1), (0, -1), (1, 0), (-1, 0))
    corners = ((1, 1), (1, -1), (-1, 1), (-1, -1))
    barrier = pltpu.get_barrier_semaphore()
    for dy, dz in faces:
        pl.semaphore_signal(barrier, inc=1, device_id=device(dy, dz), device_id_type=MESH)
    for d in range(1, nb):
        pl.semaphore_signal(barrier, inc=1, device_id={"bands": lax.rem(b + d, nb), "gy": y, "gz": z},
                            device_id_type=MESH)
    loads = [pltpu.make_async_copy(src, dst, local_sem.at[i]) for i, (src, dst) in enumerate((
        (pert_hbm, pp_ref.at[0]), (pot_hbm, pp_ref.at[1]), (orb_hbm, orb_ref), (kern_hbm, kern_ref),
        (shift_hbm, shift_ref), (occ_hbm, occ_ref)))]
    for copy in loads:
        copy.start()

    copies = []

    def remote(src, dst, to):
        n = len(copies)
        copies.append(pltpu.make_async_remote_copy(
            src_ref=src, dst_ref=dst, send_sem=send.at[n], recv_sem=recv.at[n], device_id=to, device_id_type=MESH))
        return copies[-1]

    def start(group):
        for copy in group:
            copy.start()

    def arrived(group):
        for copy in group:
            copy.wait_recv()

    def pack(dst, slot, value_of):
        for row in range(ny):
            dst[0, slot, row * w:(row + 1) * w, :] = value_of(row, 0)
            dst[1, slot, row * w:(row + 1) * w, :] = value_of(row, nz - w)

    class Border:
        def __init__(self, packed, slots, fields, own, yr, zr, cs, both):
            self.fields, self.yr, self.cs = fields, yr, cs
            rest = (ny - w) * w
            z_up = lambda at, size: remote(
                packed.at[1, slots, pl.ds(at, size)], zr.at[0, slots, pl.ds(first + at, size)], device(0, 1))
            z_down = lambda at, size: remote(
                packed.at[0, slots, pl.ds(at, size)], zr.at[1, slots, pl.ds(first + at, size)], device(0, -1))
            y_up = lambda at, size: remote(
                own(ny - w, pl.ds(at, size)), yr.at[0, slots, :, pl.ds(at, size)], device(1, 0))
            y_down = lambda at, size: remote(
                own(0, pl.ds(at, size)), yr.at[1, slots, :, pl.ds(at, size)], device(-1, 0))
            self.head = (z_up(rest, block), z_down(0, block), y_up(0, 8), y_down(nz - 8, 8))
            self.rest = (z_up(0, rest), z_down(block, rest), y_up(8, nz - 8), y_down(0, nz - 8))
            moves = (
                (zr.at[0, slots, pl.ds(first + rest, block)], zr.at[0, slots, pl.ds(top, block)], device(1, 0)),
                (zr.at[1, slots, pl.ds(first, block)], zr.at[1, slots, pl.ds(bottom, block)], device(-1, 0)),
                (cs.at[0, slots], zr.at[1, slots, pl.ds(top, block)], device(0, -1)),
                (cs.at[1, slots], zr.at[0, slots, pl.ds(bottom, block)], device(0, 1)),
            )
            self.relays = [remote(*move) for move in moves]
            if both:
                self.relays += [remote(src, dst, {**to, "bands": partner["bands"]}) for src, dst, to in moves]

        def relay(self):
            arrived(self.head)
            for field in self.fields:
                for r in range(w):
                    self.cs[0, field, r * w:(r + 1) * w, :] = self.yr[0, field, r, 0:w, :]
                    self.cs[1, field, r * w:(r + 1) * w, :] = self.yr[1, field, r, nz - w:nz, :]
            start(self.relays)

        def finish(self):
            arrived(self.rest)
            arrived(self.relays)

    pslot, vslot, kslot = orbs, orbs + 1, orbs + 2
    mine = orbs + parity
    loads[0].wait()
    pack(zs1, pslot, lambda row, at: pp_ref[0, row, at:at + w, :])
    loads[1].wait()
    pack(zs1, vslot, lambda row, at: pp_ref[1, row, at:at + w, :])
    loads[2].wait()
    for o in range(orbs):
        pack(zs1, o, lambda row, at, o=o: orb_ref[o, row, at:at + w, :])
    loads[3].wait()
    pack(zs1, kslot, lambda row, at: kern_ref[row, at:at + w, :])
    loads[4].wait()
    loads[5].wait()

    sign = 1 - 2 * parity
    partner = {"bands": b + sign, "gy": y, "gz": z}
    ysend = lax.rem(y + gy + sign, gy)
    zsend = lax.rem(z + gz + sign, gz)
    far = 1 - parity
    source_row = pl.multiple_of(far * ((ny - w) * w), 8)
    end = pl.multiple_of(top + parity * ((w + ny) * w), 8)

    everyone = pl.ds(0, orbs)
    common = Border(zs1, mine, (mine,), lambda at, zs: pp_ref.at[parity, pl.ds(at, w), zs], yr1, zr1, cs1, True)
    own = Border(zs1, everyone, range(orbs), lambda at, zs: orb_ref.at[:, pl.ds(at, w), zs], yr1, zr1, cs1, False)
    shared = [remote(ref, ref, partner) for ref in (yr1.at[:, mine], zr1.at[:, mine, pl.ds(first, ny * w)])]
    kern_moves = (
        (zs1.at[1, kslot, pl.ds(source_row, block)], zr1.at[0, kslot, pl.ds(end, block)], ysend, zsides[1]),
        (zs1.at[0, kslot, pl.ds(source_row, block)], zr1.at[1, kslot, pl.ds(end, block)], ysend, zsides[-1]),
        (zs1.at[far, kslot], zr1.at[parity, kslot, pl.ds(first, ny * w)], y, zsend),
        (kern_ref.at[pl.ds(far * (ny - w), w)], yr1.at[parity, kslot], ysend, z),
    )
    kern_copies = [remote(src, dst, {"bands": b, "gy": ty, "gz": tz}) for src, dst, ty, tz in kern_moves]
    kern_shared = [remote(dst, dst, partner) for _, dst, _, _ in kern_moves]

    def direct(packed, own, yr, zr):
        made = []
        for dy, dz in corners + faces:
            if dz:
                side, into = (1, 0) if dz == 1 else (0, 1)
                if dy == 1:
                    src, dst, size = (ny - w) * w, top, block
                elif dy == -1:
                    src, dst, size = 0, bottom, block
                else:
                    src, dst, size = 0, first, ny * w
                source = packed.at[side, everyone, pl.ds(src, size)]
                target = zr.at[into, everyone, pl.ds(dst, size)]
            else:
                into, at = (0, ny - w) if dy == 1 else (1, 0)
                source = own(at)
                target = yr.at[into, everyone]
            made.append(remote(source, target, device(dy, dz)))
        return made

    second = direct(zsu, lambda at: resp0.at[:, pl.ds(at, w)], yr2, zr2)

    pl.semaphore_wait(barrier, len(faces) + nb - 1)
    start(common.head)
    start(own.head)
    start(common.rest)
    start(own.rest)
    common.relay()
    own.relay()
    arrived(common.rest)
    start(shared)
    own.finish()
    start(kern_copies)
    arrived(common.relays)
    arrived(shared)

    low = lax.broadcasted_iota(jnp.int32, (8, nx), 0) < w

    def tiles():
        for yp in range(-1, yp_count):
            if yp >= 0:
                yield yp, 0, base + zp * yp, nz
            yield yp, 1, base + zp * yp + nz, 2 * w

    def padded(own, yr, zr, slot, yp, third):
        if third:
            row = 8 + w * yp
            return jnp.where(low, zr[1, slot, row:row + 2 * w, :], zr[0, slot, row:row + 2 * w, :])
        if yp < w:
            return yr[0, slot, yp]
        if yp >= w + ny:
            return yr[1, slot, yp - w - ny]
        return own(yp - w)

    def prepare(o):
        for yp, third, row, size in tiles():
            if o == 0:
                pv = padded(lambda r: pp_ref[0, r], yr1, zr1, pslot, yp, third)
                pbuf[row:row + size, :] = pv
            else:
                pv = pbuf[row:row + size, :]
            vv = padded(lambda r: pp_ref[1, r], yr1, zr1, vslot, yp, third)
            ov = padded(lambda r: orb_ref[o, r], yr1, zr1, o, yp, third)
            obuf[o, row:row + size, :] = ov
            fbuf[o, row:row + size, :] = ov * pv
            rbuf[o, row:row + size, :] = (RELAX / 60.0) / (32.0 / 15.0 + (vv + shift_ref[o]))

    def span(k):
        return base + zp * (k - 1) + nz, base + zp * (yp_count - k)

    def lane_sum(v):
        return pltpu.roll(v, 1, 1) + pltpu.roll(v, nx - 1, 1)

    def source60(o, row, size):
        def at(shift):
            return fbuf[o, row + shift:row + shift + size, :]
        f = at(0)
        return -30.0 * f - 5.0 * (lane_sum(f) + (at(zp) + at(-zp)) + (at(1) + at(-1)))

    def relaxed(u, o, row, size, source):
        def at(shift):
            return u[o, row + shift:row + shift + size, :]
        c = at(0)
        faces = (at(zp) + at(-zp)) + (at(1) + at(-1))
        corners = (at(zp + 1) + at(zp - 1)) + (at(1 - zp) + at(-1 - zp))
        off = 14.0 * faces + 3.0 * corners + lane_sum(14.0 * c + 3.0 * faces + corners)
        if source is not None:
            off = source + off
        return 0.2 * c + rbuf[o, row:row + size, :] * off

    def sweep(src, dst, k, o):
        for row, size in chunks(*span(k), CHUNK):
            dst[o, row:row + size, :] = relaxed(src, o, row, size, sbuf[o, row:row + size, :])

    def last(src, dst, part_ref, o, rows):
        for r in rows:
            row = base + zp * (r + w)
            value = relaxed(src, o, row, nz, sbuf[o, row:row + nz, :])
            dst[o, r] = value
            term = occ_ref[o] * obuf[o, row:row + nz, :] * value
            part_ref[r] = term if o == 0 else part_ref[r] + term

    def band_copies(src, dst, at):
        return [pltpu.make_async_remote_copy(
            src_ref=src, dst_ref=dst(d - 1), send_sem=sendb.at[at + d - 1], recv_sem=recvb.at[at + d - 1],
            device_id={"bands": lax.rem(b + d, nb), "gy": y, "gz": z}, device_id_type=MESH)
            for d in range(1, nb)]

    for o in range(orbs):
        prepare(o)
        for row, size in chunks(*span(1), CHUNK):
            s = source60(o, row, size)
            sbuf[o, row:row + size, :] = s
            ua[o, row:row + size, :] = rbuf[o, row:row + size, :] * s
        sweep(ua, ub, 2, o)
        sweep(ub, ua, 3, o)
        last(ua, resp0, part, o, range(ny))
        pack(zsu, o, lambda row, at, o=o: resp0[o, row, at:at + w, :])
    start(second)

    bands = band_copies(part, lambda d: partr.at[d], 0)
    start(bands)
    arrived(kern_copies)
    start(kern_shared)
    arrived(bands)
    for r in range(ny):
        total = part[r]
        for d in range(nb - 1):
            total = total + partr[d, r]
        row = base + zp * (r + w)
        cv = pbuf[row:row + nz, :] + kern_ref[r] * total
        for o in range(orbs):
            fbuf[o, row:row + nz, :] = obuf[o, row:row + nz, :] * cv
            ua[o, row:row + nz, :] = resp0[o, r]

    rim, at = [], 0
    for yp, third, row, size in tiles():
        if third or yp < w or yp >= w + ny:
            rim.append((yp, third, row, size, at))
            at += size
    arrived(second)
    for o in range(orbs):
        for yp, third, row, size, at in rim:
            value = padded(None, yr2, zr2, o, yp, third)
            ua[o, row:row + size, :] = value
            term = occ_ref[o] * obuf[o, row:row + size, :] * value
            hp[at:at + size, :] = term if o == 0 else hp[at:at + size, :] + term
    rims = band_copies(hp, lambda d: hpr.at[d], 2 * (nb - 1))
    start(rims)
    for o in range(orbs):
        for row, size in chunks(*span(1), CHUNK):
            ub[o, row:row + size, :] = relaxed(ua, o, row, size, None)
    arrived(kern_shared)
    arrived(rims)
    for yp, third, row, size, at in rim:
        total = hp[at:at + size, :]
        for d in range(nb - 1):
            total = total + hpr[d, at:at + size, :]
        cv = pbuf[row:row + size, :] + padded(None, yr1, zr1, kslot, yp, third) * total
        for o in range(orbs):
            fbuf[o, row:row + size, :] = obuf[o, row:row + size, :] * cv
    for o in range(orbs):
        for row, size in chunks(*span(1), CHUNK):
            s = source60(o, row, size)
            sbuf[o, row:row + size, :] = s
            ub[o, row:row + size, :] = ub[o, row:row + size, :] + rbuf[o, row:row + size, :] * s
    for o in range(orbs):
        sweep(ub, ua, 2, o)
        sweep(ua, ub, 3, o)
    for o in range(orbs):
        last(ub, respv, part2, o, range(ny))
    bands2 = band_copies(part2, lambda d: partr2.at[d], nb - 1)
    start(bands2)
    width = nx // nb
    arrived(bands2)
    for r in range(ny):
        total = part2[r]
        for d in range(nb - 1):
            total = total + partr2[d, r]
        dens_ref[r] = pltpu.roll(total, lax.rem(nx - b * width, nx), 1)[:, :width]
    for copy in copies + bands + rims + bands2:
        copy.wait_send()


def store(resp_ref, dens_ref, resp_hbm, dens_hbm, sem):
    copies = [pltpu.make_async_copy(src, dst, sem.at[i])
              for i, (src, dst) in enumerate(((resp_ref, resp_hbm), (dens_ref, dens_hbm)))]
    for copy in copies:
        copy.start()
    for copy in copies:
        copy.wait()


def on_device(counts, orbitals, orbital_shift, occupation, potential, perturbation, kernel_field):
    nb = counts[0]
    orbs, ny, nz, nx = orbitals.shape
    w = SWEEPS
    zp, yp_count = nz + 2 * w, ny + 2 * w
    rows = (nz + 2 * w) * (ny + 2 * w + 1) + 8 + 16
    rows = (rows + 7) // 8 * 8
    zrows = 8 + w * (ny + 2 * w) + 8
    f32 = jnp.float32
    vmem = lambda *shape: pltpu.VMEM(shape, f32)
    wide = vmem(orbs, rows, nx)
    tile = vmem(ny, nz, nx)
    dma = lambda n: pltpu.SemaphoreType.DMA((n,))
    remotes = 16 + 12 + 2 + 8 + 8
    rim_rows = (zp * yp_count - ny * nz) + 8
    scratch = [
        pltpu.SMEM((orbs,), f32), pltpu.SMEM((orbs,), f32),
        vmem(orbs, ny, nz, nx), vmem(2, ny, nz, nx), tile,
        vmem(2, orbs + 3, ny * w, nx), vmem(2, orbs + 3, w, nz, nx), vmem(2, orbs + 3, zrows, nx),
        vmem(2, orbs + 3, w * w, nx),
        vmem(2, orbs, ny * w, nx), vmem(2, orbs, w, nz, nx), vmem(2, orbs, zrows, nx),
        vmem(orbs, ny, nz, nx), tile, vmem(nb - 1, ny, nz, nx), tile, vmem(nb - 1, ny, nz, nx),
        vmem(rim_rows, nx), vmem(nb - 1, rim_rows, nx),
        wide, wide, wide, wide, wide, wide, vmem(rows, nx),
        dma(remotes), dma(remotes), dma(3 * (nb - 1)), dma(3 * (nb - 1)), dma(6),
    ]
    spec = pl.BlockSpec(memory_space=pltpu.VMEM)
    hbm = pl.BlockSpec(memory_space=pltpu.HBM)
    response, density = pl.pallas_call(
        functools.partial(kernel, counts),
        out_shape=(pltpu.VMEM(orbitals.shape, f32), pltpu.VMEM((ny, nz, nx // nb), f32)),
        in_specs=[hbm] * 6,
        out_specs=(spec, spec),
        scratch_shapes=scratch,
        compiler_params=pltpu.CompilerParams(
            collective_id=0, has_side_effects=True, vmem_limit_bytes=GRANT),
    )(*(pltpu.with_memory_space_constraint(array, pltpu.HBM) for array in (
        orbital_shift, occupation, orbitals, potential, perturbation, kernel_field)))
    return pl.pallas_call(
        store,
        out_shape=(jax.ShapeDtypeStruct(response.shape, f32), jax.ShapeDtypeStruct(density.shape, f32)),
        in_specs=[spec, spec],
        out_specs=(hbm, hbm),
        scratch_shapes=[dma(2)],
        compiler_params=pltpu.CompilerParams(vmem_limit_bytes=GRANT),
    )(response, density)


def solution(mesh):
    counts = (mesh.shape["bands"], mesh.shape["gy"], mesh.shape["gz"])
    placed = (
        P("bands", "gy", "gz", None),
        P("bands"),
        P("bands"),
        P("gy", "gz", None),
        P("gy", "gz", None),
        P("gy", "gz", None),
    )
    return jax.shard_map(
        functools.partial(on_device, counts),
        mesh=mesh,
        in_specs=placed,
        out_specs=(P("bands", "gy", "gz", None), P("gy", "gz", "bands")),
        check_vma=False,
    )
```

```python
import functools

import jax
import jax.numpy as jnp
from jax import lax
from jax.experimental import pallas as pl
from jax.experimental.pallas import tpu as pltpu
from jax.sharding import PartitionSpec as P

SWEEPS = 4
OUTER = 2
RELAX = 0.8
MESH = pl.DeviceIdType.MESH
CHUNK = 32
GRANT = 24 * 1024 * 1024


def chunks(start, stop, size):
    row = start
    while row < stop:
        step = min(size, stop - row)
        yield row, step
        row += step


def kernel(counts, shift_hbm, occ_hbm, orb_hbm, pot_hbm, pert_hbm, kern_hbm,
           respv, dens_ref,
           shift_ref, occ_ref, orb_ref, pp_ref, kern_ref,
           zs1, yr1, zr1, cs1, zsu, yr2, zr2, resp0, part, partr, part2, partr2, hp, hpr,
           obuf, fbuf, rbuf, sbuf, ua, ub, pbuf,
           send, recv, sendb, recvb, local_sem):
    nb, gy, gz = counts
    w = SWEEPS
    orbs, ny, nz, nx = orb_ref.shape
    zp = nz + 2 * w
    yp_count = ny + 2 * w
    base = zp + 8
    block = w * w
    first, top, bottom = 8 + block, 8, 8 + (w + ny) * w
    b = lax.axis_index("bands")
    y = lax.axis_index("gy")
    z = lax.axis_index("gz")
    parity = lax.rem(b, 2)
    ysides = {1: lax.rem(y + 1, gy), -1: lax.rem(y + gy - 1, gy), 0: y}
    zsides = {1: lax.rem(z + 1, gz), -1: lax.rem(z + gz - 1, gz), 0: z}

    def device(dy, dz):
        return {"bands": b, "gy": ysides[dy], "gz": zsides[dz]}

    faces = ((0, 1), (0, -1), (1, 0), (-1, 0))
    corners = ((1, 1), (1, -1), (-1, 1), (-1, -1))
    barrier = pltpu.get_barrier_semaphore()
    for dy, dz in faces:
        pl.semaphore_signal(barrier, inc=1, device_id=device(dy, dz), device_id_type=MESH)
    for d in range(1, nb):
        pl.semaphore_signal(barrier, inc=1, device_id={"bands": lax.rem(b + d, nb), "gy": y, "gz": z},
                            device_id_type=MESH)
    loads = [pltpu.make_async_copy(src, dst, local_sem.at[i]) for i, (src, dst) in enumerate((
        (pert_hbm, pp_ref.at[0]), (pot_hbm, pp_ref.at[1]), (orb_hbm, orb_ref), (kern_hbm, kern_ref),
        (shift_hbm, shift_ref), (occ_hbm, occ_ref)))]
    for copy in loads:
        copy.start()

    copies = []

    def remote(src, dst, to):
        n = len(copies)
        copies.append(pltpu.make_async_remote_copy(
            src_ref=src, dst_ref=dst, send_sem=send.at[n], recv_sem=recv.at[n], device_id=to, device_id_type=MESH))
        return copies[-1]

    def start(group):
        for copy in group:
            copy.start()

    def arrived(group):
        for copy in group:
            copy.wait_recv()

    def pack(dst, slot, value_of, rows=range(ny)):
        for row in rows:
            dst[0, slot, row * w:(row + 1) * w, :] = value_of(row, 0)
            dst[1, slot, row * w:(row + 1) * w, :] = value_of(row, nz - w)

    class Border:
        def __init__(self, packed, slots, fields, own, yr, zr, cs, both):
            self.fields, self.yr, self.cs = fields, yr, cs
            rest = (ny - w) * w
            z_up = lambda at, size: remote(
                packed.at[1, slots, pl.ds(at, size)], zr.at[0, slots, pl.ds(first + at, size)], device(0, 1))
            z_down = lambda at, size: remote(
                packed.at[0, slots, pl.ds(at, size)], zr.at[1, slots, pl.ds(first + at, size)], device(0, -1))
            y_up = lambda at, size: remote(
                own(ny - w, pl.ds(at, size)), yr.at[0, slots, :, pl.ds(at, size)], device(1, 0))
            y_down = lambda at, size: remote(
                own(0, pl.ds(at, size)), yr.at[1, slots, :, pl.ds(at, size)], device(-1, 0))
            self.head = (z_up(rest, block), z_down(0, block), y_up(0, 8), y_down(nz - 8, 8))
            self.rest = (z_up(0, rest), z_down(block, rest), y_up(8, nz - 8), y_down(0, nz - 8))
            moves = (
                (zr.at[0, slots, pl.ds(first + rest, block)], zr.at[0, slots, pl.ds(top, block)], device(1, 0)),
                (zr.at[1, slots, pl.ds(first, block)], zr.at[1, slots, pl.ds(bottom, block)], device(-1, 0)),
                (cs.at[0, slots], zr.at[1, slots, pl.ds(top, block)], device(0, -1)),
                (cs.at[1, slots], zr.at[0, slots, pl.ds(bottom, block)], device(0, 1)),
            )
            self.relays = [remote(*move) for move in moves]
            if both:
                self.relays += [remote(src, dst, {**to, "bands": partner["bands"]}) for src, dst, to in moves]

        def relay(self):
            arrived(self.head)
            for field in self.fields:
                for r in range(w):
                    self.cs[0, field, r * w:(r + 1) * w, :] = self.yr[0, field, r, 0:w, :]
                    self.cs[1, field, r * w:(r + 1) * w, :] = self.yr[1, field, r, nz - w:nz, :]
            start(self.relays)

        def finish(self):
            arrived(self.rest)
            arrived(self.relays)

    pslot, vslot, kslot = orbs, orbs + 1, orbs + 2
    mine = orbs + parity
    loads[0].wait()
    pack(zs1, pslot, lambda row, at: pp_ref[0, row, at:at + w, :])
    loads[1].wait()
    pack(zs1, vslot, lambda row, at: pp_ref[1, row, at:at + w, :])
    loads[2].wait()
    for o in range(orbs):
        pack(zs1, o, lambda row, at, o=o: orb_ref[o, row, at:at + w, :])
    loads[3].wait()
    pack(zs1, kslot, lambda row, at: kern_ref[row, at:at + w, :])
    loads[4].wait()
    loads[5].wait()

    sign = 1 - 2 * parity
    partner = {"bands": b + sign, "gy": y, "gz": z}
    ysend = lax.rem(y + gy + sign, gy)
    zsend = lax.rem(z + gz + sign, gz)
    far = 1 - parity
    source_row = pl.multiple_of(far * ((ny - w) * w), 8)
    end = pl.multiple_of(top + parity * ((w + ny) * w), 8)

    everyone = pl.ds(0, orbs)
    common = Border(zs1, mine, (mine,), lambda at, zs: pp_ref.at[parity, pl.ds(at, w), zs], yr1, zr1, cs1, True)
    own = Border(zs1, everyone, range(orbs), lambda at, zs: orb_ref.at[:, pl.ds(at, w), zs], yr1, zr1, cs1, False)
    shared = [remote(ref, ref, partner) for ref in (yr1.at[:, mine], zr1.at[:, mine, pl.ds(first, ny * w)])]
    kern_moves = (
        (zs1.at[1, kslot, pl.ds(source_row, block)], zr1.at[0, kslot, pl.ds(end, block)], ysend, zsides[1]),
        (zs1.at[0, kslot, pl.ds(source_row, block)], zr1.at[1, kslot, pl.ds(end, block)], ysend, zsides[-1]),
        (zs1.at[far, kslot], zr1.at[parity, kslot, pl.ds(first, ny * w)], y, zsend),
        (kern_ref.at[pl.ds(far * (ny - w), w)], yr1.at[parity, kslot], ysend, z),
    )
    kern_copies = [remote(src, dst, {"bands": b, "gy": ty, "gz": tz}) for src, dst, ty, tz in kern_moves]
    kern_shared = [remote(dst, dst, partner) for _, dst, _, _ in kern_moves]

    def direct(packed, own, yr, zr):
        made = []
        for dy, dz in corners + faces[2:] + faces[:2]:
            if dz:
                side, into = (1, 0) if dz == 1 else (0, 1)
                if dy == 1:
                    src, dst, size = (ny - w) * w, top, block
                elif dy == -1:
                    src, dst, size = 0, bottom, block
                else:
                    src, dst, size = 0, first, ny * w
                source = packed.at[side, everyone, pl.ds(src, size)]
                target = zr.at[into, everyone, pl.ds(dst, size)]
            else:
                into, at = (0, ny - w) if dy == 1 else (1, 0)
                source = own(at)
                target = yr.at[into, everyone]
            made.append(remote(source, target, device(dy, dz)))
        return made

    second = direct(zsu, lambda at: resp0.at[:, pl.ds(at, w)], yr2, zr2)

    low = lax.broadcasted_iota(jnp.int32, (8, nx), 0) < w

    def tiles():
        for yp in range(-1, yp_count):
            if yp >= 0:
                yield yp, 0, base + zp * yp, nz
            yield yp, 1, base + zp * yp + nz, 2 * w

    def padded(own, yr, zr, slot, yp, third):
        if third:
            row = 8 + w * yp
            return jnp.where(low, zr[1, slot, row:row + 2 * w, :], zr[0, slot, row:row + 2 * w, :])
        if yp < w:
            return yr[0, slot, yp]
        if yp >= w + ny:
            return yr[1, slot, yp - w - ny]
        return own(yp - w)

    def inside(yp, third):
        return not third and w <= yp < w + ny

    def prepare(o, inner):
        for yp, third, row, size in tiles():
            if inside(yp, third) != inner:
                continue
            if o == 0:
                pv = padded(lambda r: pp_ref[0, r], yr1, zr1, pslot, yp, third)
                pbuf[row:row + size, :] = pv
            else:
                pv = pbuf[row:row + size, :]
            vv = padded(lambda r: pp_ref[1, r], yr1, zr1, vslot, yp, third)
            ov = padded(lambda r: orb_ref[o, r], yr1, zr1, o, yp, third)
            obuf[o, row:row + size, :] = ov
            fbuf[o, row:row + size, :] = ov * pv
            rbuf[o, row:row + size, :] = (RELAX / 60.0) / (32.0 / 15.0 + (vv + shift_ref[o]))

    pl.semaphore_wait(barrier, len(faces) + nb - 1)
    start(common.head)
    start(own.head)
    start(common.rest)
    start(own.rest)
    for o in range(orbs):
        prepare(o, True)
    common.relay()
    own.relay()
    start(kern_copies[2:])
    arrived(common.rest)
    start(shared)
    own.finish()
    start(kern_copies[:2])
    arrived(common.relays)
    arrived(shared)

    def span(k):
        return base + zp * (k - 1) + nz, base + zp * (yp_count - k)

    def lane_sum(v):
        return pltpu.roll(v, 1, 1) + pltpu.roll(v, nx - 1, 1)

    def source60(o, row, size):
        def at(shift):
            return fbuf[o, row + shift:row + shift + size, :]
        f = at(0)
        return -30.0 * f - 5.0 * (lane_sum(f) + (at(zp) + at(-zp)) + (at(1) + at(-1)))

    def relaxed(u, o, row, size, source):
        def at(shift):
            return u[o, row + shift:row + shift + size, :]
        c = at(0)
        faces = (at(zp) + at(-zp)) + (at(1) + at(-1))
        corners = (at(zp + 1) + at(zp - 1)) + (at(1 - zp) + at(-1 - zp))
        off = 14.0 * faces + 3.0 * corners + lane_sum(14.0 * c + 3.0 * faces + corners)
        if source is not None:
            off = source + off
        return 0.2 * c + rbuf[o, row:row + size, :] * off

    def sweep(src, dst, k, o):
        for row, size in chunks(*span(k), CHUNK):
            dst[o, row:row + size, :] = relaxed(src, o, row, size, sbuf[o, row:row + size, :])

    def last(src, dst, part_ref, o, rows):
        for r in rows:
            row = base + zp * (r + w)
            value = relaxed(src, o, row, nz, sbuf[o, row:row + nz, :])
            dst[o, r] = value
            term = occ_ref[o] * obuf[o, row:row + nz, :] * value
            part_ref[r] = term if o == 0 else part_ref[r] + term

    def band_copies(src, dst, at):
        return [pltpu.make_async_remote_copy(
            src_ref=src, dst_ref=dst(d - 1), send_sem=sendb.at[at + d - 1], recv_sem=recvb.at[at + d - 1],
            device_id={"bands": lax.rem(b + d, nb), "gy": y, "gz": z}, device_id_type=MESH)
            for d in range(1, nb)]

    for o in range(orbs):
        prepare(o, False)
        for row, size in chunks(*span(1), CHUNK):
            s = source60(o, row, size)
            sbuf[o, row:row + size, :] = s
            ua[o, row:row + size, :] = rbuf[o, row:row + size, :] * s
        sweep(ua, ub, 2, o)
        sweep(ub, ua, 3, o)
    edge = [*range(w), *range(ny - w, ny)]
    for rows, group in ((edge, second[:6]), (range(w, ny - w), second[6:])):
        for o in range(orbs):
            last(ua, resp0, part, o, rows)
            pack(zsu, o, lambda row, at, o=o: resp0[o, row, at:at + w, :], rows)
        start(group)

    bands = band_copies(part, lambda d: partr.at[d], 0)
    start(bands)
    arrived(kern_copies)
    start(kern_shared)
    arrived(bands)
    for r in range(ny):
        total = part[r]
        for d in range(nb - 1):
            total = total + partr[d, r]
        row = base + zp * (r + w)
        cv = pbuf[row:row + nz, :] + kern_ref[r] * total
        for o in range(orbs):
            fbuf[o, row:row + nz, :] = obuf[o, row:row + nz, :] * cv
            ua[o, row:row + nz, :] = resp0[o, r]

    rim, parts, at = [], [], 0
    for which in (0, 1):
        begin = at
        for yp, third, row, size in tiles():
            if third == which and not inside(yp, third):
                rim.append((yp, third, row, size, at))
                at += size
        parts.append((begin, at))
    rims = []
    for which, group in ((0, second[4:6]), (1, second[:4] + second[6:])):
        arrived(group)
        for o in range(orbs):
            for yp, third, row, size, at in rim:
                if third == which:
                    value = padded(None, yr2, zr2, o, yp, third)
                    ua[o, row:row + size, :] = value
                    term = occ_ref[o] * obuf[o, row:row + size, :] * value
                    hp[at:at + size, :] = term if o == 0 else hp[at:at + size, :] + term
        begin, end_at = parts[which]
        piece = pl.ds(begin, end_at - begin)
        rims += band_copies(hp.at[piece], lambda d: hpr.at[d, piece], (2 + which) * (nb - 1))
        start(rims[which * (nb - 1):])
    for o in range(orbs):
        for row, size in chunks(*span(1), CHUNK):
            ub[o, row:row + size, :] = relaxed(ua, o, row, size, None)
    arrived(kern_shared)
    arrived(rims)
    for yp, third, row, size, at in rim:
        total = hp[at:at + size, :]
        for d in range(nb - 1):
            total = total + hpr[d, at:at + size, :]
        cv = pbuf[row:row + size, :] + padded(None, yr1, zr1, kslot, yp, third) * total
        for o in range(orbs):
            fbuf[o, row:row + size, :] = obuf[o, row:row + size, :] * cv
    for o in range(orbs):
        for row, size in chunks(*span(1), CHUNK):
            s = source60(o, row, size)
            sbuf[o, row:row + size, :] = s
            ub[o, row:row + size, :] = ub[o, row:row + size, :] + rbuf[o, row:row + size, :] * s
    for o in range(orbs):
        sweep(ub, ua, 2, o)
        sweep(ua, ub, 3, o)
    bands2, half = [], ny // 2
    for i in range(2):
        for o in range(orbs):
            last(ub, respv, part2, o, range(i * half, (i + 1) * half))
        piece = pl.ds(i * half, half)
        bands2 += band_copies(part2.at[piece], lambda d: partr2.at[d, piece], (1 + 3 * i) * (nb - 1))
        start(bands2[i * (nb - 1):])
    width = nx // nb
    for r in range(ny):
        if r % half == 0:
            arrived(bands2[r // half * (nb - 1):][:nb - 1])
        total = part2[r]
        for d in range(nb - 1):
            total = total + partr2[d, r]
        dens_ref[r] = pltpu.roll(total, lax.rem(nx - b * width, nx), 1)[:, :width]
    for copy in copies + bands + rims + bands2:
        copy.wait_send()


def store(resp_ref, dens_ref, resp_hbm, dens_hbm, sem):
    copies = [pltpu.make_async_copy(src, dst, sem.at[i])
              for i, (src, dst) in enumerate(((resp_ref, resp_hbm), (dens_ref, dens_hbm)))]
    for copy in copies:
        copy.start()
    for copy in copies:
        copy.wait()


def on_device(counts, orbitals, orbital_shift, occupation, potential, perturbation, kernel_field):
    nb = counts[0]
    orbs, ny, nz, nx = orbitals.shape
    w = SWEEPS
    zp, yp_count = nz + 2 * w, ny + 2 * w
    rows = (nz + 2 * w) * (ny + 2 * w + 1) + 8 + 16
    rows = (rows + 7) // 8 * 8
    zrows = 8 + w * (ny + 2 * w) + 8
    f32 = jnp.float32
    vmem = lambda *shape: pltpu.VMEM(shape, f32)
    wide = vmem(orbs, rows, nx)
    tile = vmem(ny, nz, nx)
    dma = lambda n: pltpu.SemaphoreType.DMA((n,))
    remotes = 16 + 12 + 2 + 8 + 8
    rim_rows = (zp * yp_count - ny * nz) + 8
    scratch = [
        pltpu.SMEM((orbs,), f32), pltpu.SMEM((orbs,), f32),
        vmem(orbs, ny, nz, nx), vmem(2, ny, nz, nx), tile,
        vmem(2, orbs + 3, ny * w, nx), vmem(2, orbs + 3, w, nz, nx), vmem(2, orbs + 3, zrows, nx),
        vmem(2, orbs + 3, w * w, nx),
        vmem(2, orbs, ny * w, nx), vmem(2, orbs, w, nz, nx), vmem(2, orbs, zrows, nx),
        vmem(orbs, ny, nz, nx), tile, vmem(nb - 1, ny, nz, nx), tile, vmem(nb - 1, ny, nz, nx),
        vmem(rim_rows, nx), vmem(nb - 1, rim_rows, nx),
        wide, wide, wide, wide, wide, wide, vmem(rows, nx),
        dma(remotes), dma(remotes), dma(5 * (nb - 1)), dma(5 * (nb - 1)), dma(6),
    ]
    spec = pl.BlockSpec(memory_space=pltpu.VMEM)
    hbm = pl.BlockSpec(memory_space=pltpu.HBM)
    response, density = pl.pallas_call(
        functools.partial(kernel, counts),
        out_shape=(pltpu.VMEM(orbitals.shape, f32), pltpu.VMEM((ny, nz, nx // nb), f32)),
        in_specs=[hbm] * 6,
        out_specs=(spec, spec),
        scratch_shapes=scratch,
        compiler_params=pltpu.CompilerParams(
            collective_id=0, has_side_effects=True, vmem_limit_bytes=GRANT),
    )(*(pltpu.with_memory_space_constraint(array, pltpu.HBM) for array in (
        orbital_shift, occupation, orbitals, potential, perturbation, kernel_field)))
    return pl.pallas_call(
        store,
        out_shape=(jax.ShapeDtypeStruct(response.shape, f32), jax.ShapeDtypeStruct(density.shape, f32)),
        in_specs=[spec, spec],
        out_specs=(hbm, hbm),
        scratch_shapes=[dma(2)],
        compiler_params=pltpu.CompilerParams(vmem_limit_bytes=GRANT),
    )(response, density)


def solution(mesh):
    counts = (mesh.shape["bands"], mesh.shape["gy"], mesh.shape["gz"])
    placed = (
        P("bands", "gy", "gz", None),
        P("bands"),
        P("bands"),
        P("gy", "gz", None),
        P("gy", "gz", None),
        P("gy", "gz", None),
    )
    return jax.shard_map(
        functools.partial(on_device, counts),
        mesh=mesh,
        in_specs=placed,
        out_specs=(P("bands", "gy", "gz", None), P("gy", "gz", "bands")),
        check_vma=False,
    )
```
